32 devices in a mesh: groups: 2 (over y), seg: 4 (over z), ch: 2 (over x), sub: 2 (over core).
Axes of the slice: x: 2, y: 2, z: 4, core: 2. Of those that a mesh axis runs over, the one named last changes fastest.
Arguments:
- rank_series: bfloat16 [2048, 16384], P(('groups', 'ch', 'sub'), 'seg'), parts along dimension 0, may hold values from -6 to 6
- power_series: bfloat16 [2048, 16384], P(('groups', 'ch', 'sub'), 'seg'), parts along dimension 0, may hold values from -6 to 6
- seg_offsets: int32 [32], P(('groups', 'seg')), parts along dimension 0, may hold values from 2048 to 4095, as said below
- bin_index: int32 [128], replicated, may hold values from 0 to 511, as said below
Outputs:
- cross_spectra: bfloat16 [2, 256, 1024, 1024], P(None, ('groups', 'seg'), ('ch', 'sub')), parts along dimension 1
The draws below stay inside these ranges and needn't reach their ends.
There are 2 independent parts, one for each index of `groups`. The reference program is written for one: setup_inputs(seed, part) draws one part's arguments, and reference() takes and returns one part's arrays. A program takes and returns all parts, laid end to end along the dimension named above; an argument that names none is the same for every part. Nothing has to cross between parts.
Inputs may be any that keep to these rules, and one draw needn't show every extreme that they name: `seg_offsets`: every segment reads at least half of its samples past its own 4096 samples, in the following ones. `bin_index`: the bins are distinct.
All inputs are finite; a program needn't handle non-finite values.
Results may differ from the reference program's by a relative error of at most 0.0055.
Values may be sent and summed in bfloat16 or wider, within the bound.
A program may use at most 192 MiB of HBM per device.

```python
import math
import jax
import jax.numpy as jnp
from jax import lax

R = 1024
P_SIZE = 1024
LEN = 4096
BINS = 128
SEG_DEV = 4
SEGS = 16
SAMPLES = 16384


def draw_seg_offsets(key, part):
    values = jax.random.randint(key, (SEGS,), LEN // 2, LEN, dtype=jnp.int32)
    return values.at[0].set(LEN - 1).at[1].set(LEN // 2)


def draw_bin_index(key, part):
    shuffled = jax.random.permutation(key, 4 * BINS - 2).astype(jnp.int32) + 1
    ends = jnp.array([0, 4 * BINS - 1], dtype=jnp.int32)
    return jnp.concatenate([ends, shuffled[:BINS - 2]])


def steps_of(stream_key, extent, split, smallest, largest):
    gain = 1.0
    for dim, shards_of in split:
        steps = jax.random.uniform(jax.random.fold_in(jax.random.fold_in(stream_key, 6), dim), (shards_of,), jnp.float32, smallest / len(split), largest / len(split))
        gain = gain * jnp.repeat(jnp.exp(steps), extent[dim] // shards_of).reshape((-1,) + (1,) * (len(extent) - 1 - dim))
    return gain


def bell_draw(rng, shape, spread, bound, split=(), held_as=jnp.bfloat16):
    loudness = steps_of(rng, shape, split, -0.22, 0.18) if split else 1.0
    drawn = jax.random.normal(rng, shape, jnp.float32) * spread * loudness
    return jnp.minimum(jnp.maximum(drawn, -bound), bound).astype(held_as)


def setup_inputs(seed: int = 0, part: int = 0) -> dict:
    streams_of = jax.random.split(jax.random.key(seed), 5)
    part_splits = jax.random.split(jax.random.fold_in(streams_of[4], part), 5)
    rank_series = bell_draw(part_splits[0], (R, SAMPLES), 1.0, 6.0, ((0, 4), (1, 4)))
    power_series = bell_draw(part_splits[1], (P_SIZE, SAMPLES), 1.0, 6.0, ((0, 4), (1, 4)))
    seg_offsets = draw_seg_offsets(jax.random.fold_in(jax.random.fold_in(streams_of[4], part), 71), part)
    bin_index = draw_bin_index(jax.random.fold_in(streams_of[4], 71), part)
    return dict(rank_series=rank_series, power_series=power_series, seg_offsets=seg_offsets, bin_index=bin_index)


def make_kernel(bin_index):
    sample_ids = jnp.arange(LEN, dtype=jnp.int32)
    window = 0.5 - 0.5 * jnp.cos((2.0 * math.pi / LEN) * sample_ids.astype(jnp.float32))
    phase = (bin_index.astype(jnp.int32)[:, None] * sample_ids[None, :]) % LEN
    angle = (2.0 * math.pi / LEN) * phase.astype(jnp.float32)
    factor = (3.0 * LEN / 8.0) ** -0.5
    waves = jnp.stack([jnp.cos(angle), -jnp.sin(angle)]) * factor
    return (waves * window).astype(jnp.bfloat16)


def reference(rank_series, power_series, seg_offsets, bin_index):
    kernel = make_kernel(bin_index).astype(jnp.float32)
    starts = (jnp.arange(SEGS, dtype=jnp.int32) // SEG_DEV) * LEN + seg_offsets.astype(jnp.int32)

    def spectra(series):
        padded = jnp.concatenate([series, jnp.zeros((series.shape[0], LEN), series.dtype)], axis=1)

        def one_segment(start):
            segment = lax.dynamic_slice_in_dim(padded, start, LEN, 1).astype(jnp.float32)
            return jnp.einsum("tkn,cn->tkc", kernel, segment, precision=lax.Precision.HIGHEST)

        return lax.map(one_segment, starts).astype(jnp.bfloat16)

    rank_spectra = spectra(rank_series).astype(jnp.float32)
    power_spectra = spectra(power_series).astype(jnp.float32)
    swapped = jnp.stack([power_spectra[:, 1], -power_spectra[:, 0]], axis=1)
    real_part = jnp.einsum("gtkr,gtkp->krp", rank_spectra, power_spectra)
    imag_part = jnp.einsum("gtkr,gtkp->krp", rank_spectra, swapped)
    return jnp.stack([real_part, imag_part]).astype(jnp.bfloat16)
```

```python
import functools
import math

import jax
import jax.numpy as jnp
from jax import lax
from jax.experimental import pallas as pl
from jax.experimental.pallas import tpu as pltpu
from jax.sharding import PartitionSpec as P

LANES = 128
FINE = 64
POWER, RANK = 0, 1
HEAD, OWN = 0, 1


def waves_of(freq, samples, length):
    phase = jnp.bitwise_and(freq * samples, length - 1)
    angle = 2.0 * math.pi / length * phase.astype(jnp.float32)
    return jnp.cos(angle), jnp.sin(angle)


def build_table(length, bins_ref, coarse, table):
    bins = bins_ref.shape[-1]
    pad = length // 2
    factor = (3.0 * length / 8.0) ** (-0.5)
    rows = length // FINE
    fine = lax.broadcasted_iota(jnp.int32, (FINE, bins), 0)
    steps = lax.broadcasted_iota(jnp.int32, (rows, bins), 0) * FINE
    freq = bins_ref[...]
    cb, sb = waves_of(freq, fine, length)
    cv, sv = waves_of(1, fine, length)
    cv, sv = cv * (0.5 * factor), sv * (0.5 * factor)
    coarse[0], coarse[1] = waves_of(freq, steps, length)
    coarse[2], coarse[3] = waves_of(1, steps, length)

    @pl.loop(0, rows)
    def _(a):
        ca = coarse[0, pl.ds(a, 1), :]
        sa = coarse[1, pl.ds(a, 1), :]
        cw = coarse[2, pl.ds(a, 1), :]
        sw = coarse[3, pl.ds(a, 1), :]
        window = 0.5 * factor - (cw * cv - sw * sv)
        at = pl.ds(pl.multiple_of(pad + a * FINE, FINE), FINE)
        table[0, at, :] = (ca * cb - sa * sb) * window
        table[1, at, :] = -(sa * cb + ca * sb) * window

    @pl.loop(0, pad // FINE)
    def _(a):
        for t in range(2):
            for base in (0, pad + length):
                at = pl.ds(pl.multiple_of(base + a * FINE, FINE), FINE)
                table[t, at, :] = jnp.zeros((FINE, bins), jnp.float32)


def transform(length, side, chunk, table, offset, series, acc, stage, s):
    bins = table.shape[-1]
    first = 0 if side == HEAD else length // 2
    offset = jnp.minimum(jnp.maximum(offset, length // 2), length)
    shift = (length if side == HEAD else 0) + length // 2 - offset
    acc[...] = jnp.zeros_like(acc)

    @pl.loop(0, (length - first) // chunk)
    def _(c):
        col = pl.multiple_of(first + c * chunk, chunk)
        at = pl.ds(col + shift, chunk)
        waves = jnp.concatenate(
            [table[0, at, :].astype(jnp.bfloat16), table[1, at, :].astype(jnp.bfloat16)], axis=1
        )
        acc[...] += jnp.dot(series[:, pl.ds(col, chunk)], waves, preferred_element_type=jnp.float32)

    for t in range(2):
        for l in range(acc.shape[0] // LANES):
            lanes = slice(l * LANES, (l + 1) * LANES)
            stage[side, s, t, l] = acc[lanes, t * bins : (t + 1) * bins].T


def exchange_kernel(
    length, chunk, peers, plane, bins_ref, offs_ref, rank_hbm, power_hbm,
    power_all, rank_owned, coarse, table, acc, stage, offs_in, series,
    near, from_above, from_below, summed,
    load_sem, offs_sem, near_send, above_recv, below_recv, far_send, far_recv, plane_send, plane_recv,
):
    mesh_id = pl.DeviceIdType.MESH
    here = lax.axis_index("seg")
    above = lax.rem(here + 1, peers)
    below = lax.rem(here + peers - 1, peers)
    fanout = plane[0] * plane[1]
    place = lax.axis_index("ch") * plane[1] + lax.axis_index("sub")
    segs, _, block, width = summed.shape[2:]
    top = here == peers - 1
    has_head = here > 0

    loads = [
        pltpu.make_async_copy(power_hbm, series.at[pl.ds(0, width)], load_sem.at[0]),
        pltpu.make_async_copy(rank_hbm, series.at[pl.ds(width, width)], load_sem.at[1]),
    ]
    for load in loads:
        load.start()

    def beside(q):
        return {"ch": q // plane[1], "sub": lax.rem(q, plane[1])}

    barrier = pltpu.get_barrier_semaphore()
    for i in range(1, peers):
        pl.semaphore_signal(
            barrier, inc=1, device_id={"seg": lax.rem(here + i, peers)}, device_id_type=mesh_id
        )
    for i in range(1, fanout):
        pl.semaphore_signal(
            barrier, inc=1, device_id=beside(lax.rem(place + i, fanout)), device_id_type=mesh_id
        )

    build_table(length, bins_ref, coarse, table)
    pl.semaphore_wait(barrier, peers + fanout - 2)

    offs_copy = pltpu.make_async_remote_copy(
        src_ref=offs_ref,
        dst_ref=offs_in,
        send_sem=offs_sem.at[0],
        recv_sem=offs_sem.at[1],
        device_id={"seg": above},
        device_id_type=mesh_id,
    )

    def near_copy(kind, owner, s, up):
        return pltpu.make_async_remote_copy(
            src_ref=near.at[kind, owner, s],
            dst_ref=(from_below if up else from_above).at[kind, owner, s],
            send_sem=near_send.at[kind, owner, s],
            recv_sem=(below_recv if up else above_recv).at[kind, owner, s],
            device_id={"seg": above if up else below},
            device_id_type=mesh_id,
        )

    def slot(kind, group):
        return power_all.at[place, group] if kind == POWER else rank_owned.at[group]

    def far_copy(kind, owner, group):
        return pltpu.make_async_remote_copy(
            src_ref=summed.at[kind, owner],
            dst_ref=slot(kind, group),
            send_sem=far_send.at[kind, owner],
            recv_sem=far_recv.at[kind, group],
            device_id={"seg": owner},
            device_id_type=mesh_id,
        )

    def plane_copy(group, sender, target):
        return pltpu.make_async_remote_copy(
            src_ref=power_all.at[sender, group],
            dst_ref=power_all.at[sender, group],
            send_sem=plane_send.at[group, target],
            recv_sem=plane_recv.at[group, sender],
            device_id=beside(target),
            device_id_type=mesh_id,
        )

    def forward(group):
        for i in range(1, fanout):
            plane_copy(group, place, lax.rem(place + i, fanout)).start()

    def piece(side, kind, owner, s, t):
        rows = pl.ds(pl.multiple_of(owner * block, block), block)
        per = width // LANES
        return jnp.concatenate([stage[side, s, t, kind * per + l, rows, :] for l in range(per)], axis=1)

    def send_near(side, kind, owner, s):
        for t in range(2):
            near[kind, owner, s, t] = piece(side, kind, owner, s, t).astype(near.dtype)
        near_copy(kind, owner, s, side == OWN).start()

    def near_wait(kind, owner, up):
        for s in range(segs):
            near_copy(kind, owner, s, up).wait_recv()

    def total(side, kind, owner, late, out):
        for s in range(segs):
            for t in range(2):
                value = piece(side, kind, owner, s, t)
                if late is not None:
                    value = value + late[kind, owner, s, t].astype(jnp.float32)
                out[s, t] = value.astype(out.dtype)

    def own_total(kind, owner, out):
        @pl.when(jnp.logical_not(top))
        def _():
            near_wait(kind, owner, False)
            total(OWN, kind, owner, from_above, out)

        @pl.when(top)
        def _():
            total(OWN, kind, owner, None, out)

    def head_total(kind, owner, out):
        near_wait(kind, owner, True)
        total(HEAD, kind, owner, from_below, out)

    def each(low, high, step):
        lax.fori_loop(low, high, lambda d, _: step(d), None)

    def farther(kind, s):
        each(0, here - 1, lambda d: send_near(HEAD, kind, d, s))

    def nearest(kind):
        @pl.when(has_head)
        def _():
            for s in range(segs):
                send_near(HEAD, kind, here - 1, s)

    def upward(kind, s):
        each(0, peers - 1 - here, lambda i: send_near(OWN, kind, peers - 1 - i, s))

    @pl.when(jnp.logical_not(top))
    def _():
        offs_copy.start()

    for load in loads:
        load.wait()

    @pl.when(has_head)
    def _():
        offs_copy.wait_recv()
        for s in range(segs):
            transform(length, HEAD, chunk, table, offs_in[s], series, acc, stage, s)
            farther(POWER, s)
        nearest(POWER)

    for s in range(segs):
        transform(length, OWN, chunk, table, offs_ref[s], series, acc, stage, s)
        upward(POWER, s)

    def totals(kind):
        def down(d):
            own_total(kind, d, summed.at[kind, d])
            far_copy(kind, d, here).start()

        def up(i):
            d = peers - 1 - i
            head_total(kind, d, summed.at[kind, d])
            far_copy(kind, d, below).start()

        @pl.when(top)
        def _():
            down(here - 1)

        each(0, jnp.where(top, here - 1, here), down)
        each(0, jnp.where(has_head, peers - 1 - here, 0), up)

    def local(kind):
        own_total(kind, here, slot(kind, here))
        if kind == POWER:
            forward(here)

        @pl.when(has_head)
        def _():
            head_total(kind, here, slot(kind, here - 1))
            if kind == POWER:
                forward(here - 1)

    def others(step):
        each(here + 1, peers, step)
        each(2, here + 1, lambda i: step(here - i))

    def arrived(group):
        far_copy(POWER, here, group).wait_recv()
        forward(group)

    totals(POWER)
    for s in range(segs):
        farther(RANK, s)
        upward(RANK, s)
    nearest(RANK)
    local(POWER)
    others(arrived)
    totals(RANK)
    local(RANK)
    others(lambda group: far_copy(RANK, here, group).wait_recv())

    def gathered(group):
        for i in range(1, fanout):
            other = lax.rem(place + i, fanout)
            plane_copy(group, other, place).wait_recv()
            plane_copy(group, place, other).wait_send()

    each(0, peers, gathered)

    def drained(d):
        for kind in range(2):
            @pl.when(d != here)
            def _():
                for s in range(segs):
                    near_copy(kind, d, s, True).wait_send()

            @pl.when((d < here) | ((d > here) & has_head))
            def _():
                far_copy(kind, d, 0).wait_send()

    each(0, peers, drained)

    @pl.when(jnp.logical_not(top))
    def _():
        offs_copy.wait_send()


def exchange(bin_index, seg_offsets, rank_series, power_series):
    width, length = rank_series.shape
    bins = bin_index.shape[0]
    segs = seg_offsets.shape[0]
    peers = lax.axis_size("seg")
    plane = (lax.axis_size("ch"), lax.axis_size("sub"))
    fanout = plane[0] * plane[1]
    shape = (segs, 2, bins // peers, width)
    vmem = pl.BlockSpec(memory_space=pltpu.VMEM)
    smem = pl.BlockSpec(memory_space=pltpu.SMEM)
    hbm = pl.BlockSpec(memory_space=pl.ANY)
    dma = pltpu.SemaphoreType.DMA
    return pl.pallas_call(
        functools.partial(exchange_kernel, length, 1024, peers, plane),
        out_shape=(
            jax.ShapeDtypeStruct((fanout, peers) + shape, jnp.bfloat16),
            jax.ShapeDtypeStruct((peers,) + shape, jnp.bfloat16),
        ),
        in_specs=[vmem, smem, hbm, hbm],
        out_specs=(vmem, vmem),
        scratch_shapes=[
            pltpu.VMEM((4, length // FINE, bins), jnp.float32),
            pltpu.VMEM((2, 2 * length, bins), jnp.float32),
            pltpu.VMEM((2 * width, 2 * bins), jnp.float32),
            pltpu.VMEM((2, segs, 2, 2 * width // LANES, bins, LANES), jnp.float32),
            pltpu.SMEM((segs,), jnp.int32),
            pltpu.VMEM((2 * width, length), jnp.bfloat16),
        ]
        + [pltpu.VMEM((2, peers) + shape, jnp.bfloat16)] * 4
        + [dma((2,)), dma((2,))]
        + [dma((2, peers, segs))] * 3
        + [dma((2, peers))] * 2
        + [dma((peers, fanout))] * 2,
        compiler_params=pltpu.CompilerParams(
            vmem_limit_bytes=56 << 20, collective_id=0, has_side_effects=True
        ),
        name="exchange_spectra",
    )(bin_index[None, :], seg_offsets, rank_series, power_series)


def cross_kernel(step, rank_ref, power_ref, out_hbm, wide, stage, sem):
    gathered, depth, block, width = power_ref.shape
    per = width // LANES
    pad = wide.shape[1] // depth

    @pl.loop(0, depth)
    def _(e):
        at = pl.ds(pl.multiple_of(e * pad, 8), block)
        for l in range(per):
            lanes = slice(l * LANES, (l + 1) * LANES)
            wide[l, at, :] = rank_ref[e, :, lanes].astype(jnp.float32)
            for d in range(gathered):
                wide[per * (1 + d) + l, at, :] = power_ref[d, e, :, lanes].astype(jnp.float32)

    def copy(i):
        return pltpu.make_async_copy(stage.at[i], out_hbm.at[:, i], sem.at[i])

    def rows(first, i, t):
        return jnp.concatenate(
            [wide[first + l, pl.ds(i + t * pad, depth // 2, stride=2 * pad), :] for l in range(per)], axis=1
        )

    @pl.loop(0, block // step)
    def _(b):
        for j in range(step):
            i = b * step + j
            re, im = rows(0, i, 0), rows(0, i, 1)
            both = jnp.concatenate(
                [jnp.concatenate([re, -im], axis=1), jnp.concatenate([im, re], axis=1)], axis=0
            ).astype(jnp.bfloat16)
            for d in range(gathered):
                first = per * (1 + d)
                power = jnp.concatenate([rows(first, i, 0), rows(first, i, 1)], axis=0)
                sums = lax.dot_general(
                    both,
                    power.astype(jnp.bfloat16),
                    (((0,), (0,)), ((), ())),
                    preferred_element_type=jnp.float32,
                ).astype(stage.dtype)
                stage[i, 0, :, d * width : (d + 1) * width] = sums[:width]
                stage[i, 1, :, d * width : (d + 1) * width] = sums[width:]
            copy(i).start()

    @pl.loop(0, block)
    def _(i):
        copy(i).wait()


def cross(rank_owned, power_all):
    gathered, peers, segs, _, bins, width = power_all.shape
    depth = 2 * peers * segs
    pad = -(-bins // 8) * 8 + 8
    vmem = pl.BlockSpec(memory_space=pltpu.VMEM)
    return pl.pallas_call(
        functools.partial(cross_kernel, min(8, bins)),
        out_shape=jax.ShapeDtypeStruct((2, bins, width, gathered * width), jnp.bfloat16),
        in_specs=[vmem, vmem],
        out_specs=pl.BlockSpec(memory_space=pl.ANY),
        scratch_shapes=[
            pltpu.VMEM(((1 + gathered) * width // LANES, depth * pad, LANES), jnp.float32),
            pltpu.VMEM((bins, 2, width, gathered * width), jnp.bfloat16),
            pltpu.SemaphoreType.DMA((bins,)),
        ],
        compiler_params=pltpu.CompilerParams(vmem_limit_bytes=56 << 20),
        name="cross_spectra",
    )(rank_owned.reshape(depth, bins, width), power_all.reshape(gathered, depth, bins, width))


def body(rank_series, power_series, seg_offsets, bin_index):
    power_all, rank_owned = exchange(bin_index, seg_offsets, rank_series, power_series)
    return cross(rank_owned, power_all)


def solution(mesh):
    return jax.shard_map(
        body,
        mesh=mesh,
        in_specs=(
            P(("groups", "ch", "sub"), "seg"),
            P(("groups", "ch", "sub"), "seg"),
            P(("groups", "seg")),
            P(),
        ),
        out_specs=P(None, ("groups", "seg"), ("ch", "sub"), None),
        check_vma=False,
    )
```

```python
import functools
import math

import jax
import jax.numpy as jnp
from jax import lax
from jax.experimental import pallas as pl
from jax.experimental.pallas import tpu as pltpu
from jax.sharding import PartitionSpec as P

LANES = 128
FINE = 64
POWER, RANK = 0, 1
HEAD, OWN = 0, 1


def waves_of(freq, samples, length):
    phase = jnp.bitwise_and(freq * samples, length - 1)
    angle = 2.0 * math.pi / length * phase.astype(jnp.float32)
    return jnp.cos(angle), jnp.sin(angle)


def build_table(length, bins_ref, coarse, table):
    bins = bins_ref.shape[-1]
    pad = length // 2
    factor = (3.0 * length / 8.0) ** (-0.5)
    rows = length // FINE
    fine = lax.broadcasted_iota(jnp.int32, (FINE, bins), 0)
    steps = lax.broadcasted_iota(jnp.int32, (rows, bins), 0) * FINE
    freq = bins_ref[...]
    cb, sb = waves_of(freq, fine, length)
    cv, sv = waves_of(1, fine, length)
    cv, sv = cv * (0.5 * factor), sv * (0.5 * factor)
    coarse[0], coarse[1] = waves_of(freq, steps, length)
    coarse[2], coarse[3] = waves_of(1, steps, length)

    @pl.loop(0, rows)
    def _(a):
        ca = coarse[0, pl.ds(a, 1), :]
        sa = coarse[1, pl.ds(a, 1), :]
        cw = coarse[2, pl.ds(a, 1), :]
        sw = coarse[3, pl.ds(a, 1), :]
        window = 0.5 * factor - (cw * cv - sw * sv)
        at = pl.ds(pl.multiple_of(pad + a * FINE, FINE), FINE)
        table[0, at, :] = (ca * cb - sa * sb) * window
        table[1, at, :] = -(sa * cb + ca * sb) * window

    @pl.loop(0, pad // FINE)
    def _(a):
        for t in range(2):
            for base in (0, pad + length):
                at = pl.ds(pl.multiple_of(base + a * FINE, FINE), FINE)
                table[t, at, :] = jnp.zeros((FINE, bins), jnp.float32)


def transform(length, side, chunk, table, offset, series, acc, stage, s):
    bins = table.shape[-1]
    first = 0 if side == HEAD else length // 2
    offset = jnp.minimum(jnp.maximum(offset, length // 2), length)
    shift = (length if side == HEAD else 0) + length // 2 - offset
    acc[...] = jnp.zeros_like(acc)

    @pl.loop(0, (length - first) // chunk)
    def _(c):
        col = pl.multiple_of(first + c * chunk, chunk)
        at = pl.ds(col + shift, chunk)
        waves = jnp.concatenate(
            [table[0, at, :].astype(jnp.bfloat16), table[1, at, :].astype(jnp.bfloat16)], axis=1
        )
        acc[...] += jnp.dot(series[:, pl.ds(col, chunk)], waves, preferred_element_type=jnp.float32)

    for t in range(2):
        for l in range(acc.shape[0] // LANES):
            lanes = slice(l * LANES, (l + 1) * LANES)
            stage[side, s, t, l] = acc[lanes, t * bins : (t + 1) * bins].T


def exchange_kernel(
    length, chunk, peers, plane, bins_ref, offs_ref, rank_hbm, power_hbm,
    power_all, rank_owned, coarse, table, acc, stage, offs_in, series,
    near, from_above, from_below, summed,
    load_sem, offs_sem, near_send, above_recv, below_recv, far_send, far_recv, plane_send, plane_recv,
):
    mesh_id = pl.DeviceIdType.MESH
    here = lax.axis_index("seg")
    above = lax.rem(here + 1, peers)
    below = lax.rem(here + peers - 1, peers)
    fanout = plane[0] * plane[1]
    place = lax.axis_index("ch") * plane[1] + lax.axis_index("sub")
    segs, _, block, width = summed.shape[2:]
    top = here == peers - 1
    has_head = here > 0

    loads = [
        pltpu.make_async_copy(power_hbm, series.at[pl.ds(0, width)], load_sem.at[0]),
        pltpu.make_async_copy(rank_hbm, series.at[pl.ds(width, width)], load_sem.at[1]),
    ]
    for load in loads:
        load.start()

    def beside(q):
        return {"ch": q // plane[1], "sub": lax.rem(q, plane[1])}

    barrier = pltpu.get_barrier_semaphore()
    for i in range(1, peers):
        pl.semaphore_signal(
            barrier, inc=1, device_id={"seg": lax.rem(here + i, peers)}, device_id_type=mesh_id
        )
    for i in range(1, fanout):
        pl.semaphore_signal(
            barrier, inc=1, device_id=beside(lax.rem(place + i, fanout)), device_id_type=mesh_id
        )

    build_table(length, bins_ref, coarse, table)
    for load in loads:
        load.wait()
    for s in range(segs // 2):
        transform(length, OWN, chunk, table, offs_ref[s], series, acc, stage, s)
    pl.semaphore_wait(barrier, peers + fanout - 2)

    offs_copy = pltpu.make_async_remote_copy(
        src_ref=offs_ref,
        dst_ref=offs_in,
        send_sem=offs_sem.at[0],
        recv_sem=offs_sem.at[1],
        device_id={"seg": above},
        device_id_type=mesh_id,
    )

    def near_copy(kind, owner, s, up):
        return pltpu.make_async_remote_copy(
            src_ref=near.at[kind, owner, s],
            dst_ref=(from_below if up else from_above).at[kind, owner, s],
            send_sem=near_send.at[kind, owner, s],
            recv_sem=(below_recv if up else above_recv).at[kind, owner, s],
            device_id={"seg": above if up else below},
            device_id_type=mesh_id,
        )

    def slot(kind, group):
        return power_all.at[place, group] if kind == POWER else rank_owned.at[group]

    def far_copy(kind, owner, group):
        return pltpu.make_async_remote_copy(
            src_ref=summed.at[kind, owner],
            dst_ref=slot(kind, group),
            send_sem=far_send.at[kind, owner],
            recv_sem=far_recv.at[kind, group],
            device_id={"seg": owner},
            device_id_type=mesh_id,
        )

    def plane_copy(group, sender, target, lane):
        return pltpu.make_async_remote_copy(
            src_ref=power_all.at[sender, group],
            dst_ref=power_all.at[sender, group],
            send_sem=plane_send.at[group, lane],
            recv_sem=plane_recv.at[group, sender],
            device_id=beside(target),
            device_id_type=mesh_id,
        )

    my_ch, my_sub = lax.axis_index("ch"), lax.axis_index("sub")
    chs = [lax.rem(my_ch + i, plane[0]) * plane[1] for i in range(1, plane[0])]
    subs = [lax.rem(my_sub + i, plane[1]) for i in range(1, plane[1])]
    column = my_ch * plane[1]

    def forward(group):
        for target in [c + my_sub for c in chs] + [column + q for q in subs]:
            plane_copy(group, place, target, target).start()

    def piece(side, kind, owner, s, t):
        rows = pl.ds(pl.multiple_of(owner * block, block), block)
        per = width // LANES
        return jnp.concatenate([stage[side, s, t, kind * per + l, rows, :] for l in range(per)], axis=1)

    def send_near(side, kind, owner, s):
        for t in range(2):
            near[kind, owner, s, t] = piece(side, kind, owner, s, t).astype(near.dtype)
        near_copy(kind, owner, s, side == OWN).start()

    def near_wait(kind, owner, up):
        for s in range(segs):
            near_copy(kind, owner, s, up).wait_recv()

    def total(side, kind, owner, late, out):
        for s in range(segs):
            for t in range(2):
                value = piece(side, kind, owner, s, t)
                if late is not None:
                    value = value + late[kind, owner, s, t].astype(jnp.float32)
                out[s, t] = value.astype(out.dtype)

    def own_total(kind, owner, out):
        @pl.when(jnp.logical_not(top))
        def _():
            near_wait(kind, owner, False)
            total(OWN, kind, owner, from_above, out)

        @pl.when(top)
        def _():
            total(OWN, kind, owner, None, out)

    def head_total(kind, owner, out):
        near_wait(kind, owner, True)
        total(HEAD, kind, owner, from_below, out)

    def each(low, high, step):
        lax.fori_loop(low, high, lambda d, _: step(d), None)

    def downward(high, s):
        for kind in range(2):
            each(0, high, lambda d: send_near(HEAD, kind, d, s))

    def upward(s):
        for kind in range(2):
            each(0, peers - 1 - here, lambda i: send_near(OWN, kind, peers - 1 - i, s))

    @pl.when(jnp.logical_not(top))
    def _():
        offs_copy.start()

    for s in range(segs // 2, segs):
        transform(length, OWN, chunk, table, offs_ref[s], series, acc, stage, s)

    def total_down(kind, d):
        own_total(kind, d, summed.at[kind, d])
        far_copy(kind, d, here).start()

    def total_up(kind, i):
        d = peers - 1 - i
        head_total(kind, d, summed.at[kind, d])
        far_copy(kind, d, below).start()

    @pl.when(top)
    def _():
        each(0, here - 1, functools.partial(total_down, POWER))

    for s in range(segs):
        upward(s)

    @pl.when(has_head)
    def _():
        offs_copy.wait_recv()
        for s in range(segs):
            transform(length, HEAD, chunk, table, offs_in[s], series, acc, stage, s)
            downward(jnp.where(top, here - 1, here), s)

        @pl.when(top)
        def _():
            for kind in range(2):
                for s in range(segs):
                    send_near(HEAD, kind, here - 1, s)
            for kind in range(2):
                total_down(kind, here - 1)

    each(0, jnp.where(top, 0, here), functools.partial(total_down, POWER))
    each(0, jnp.where(has_head, peers - 1 - here, 0), functools.partial(total_up, POWER))
    each(0, jnp.where(top, here - 1, here), functools.partial(total_down, RANK))
    each(0, jnp.where(has_head, peers - 1 - here, 0), functools.partial(total_up, RANK))

    def local(kind):
        own_total(kind, here, slot(kind, here))
        if kind == POWER:
            forward(here)

        @pl.when(has_head)
        def _():
            head_total(kind, here, slot(kind, here - 1))
            if kind == POWER:
                forward(here - 1)

    def others(step):
        each(here + 1, peers, step)
        each(2, here + 1, lambda i: step(here - i))

    def arrived(group):
        far_copy(POWER, here, group).wait_recv()
        forward(group)

    local(POWER)
    others(arrived)
    local(RANK)
    others(lambda group: far_copy(RANK, here, group).wait_recv())

    def relayed(group):
        for c in chs:
            plane_copy(group, c + my_sub, place, 0).wait_recv()
            for q in subs:
                plane_copy(group, c + my_sub, column + q, c + q).start()

    def gathered(group):
        for q in subs:
            plane_copy(group, column + q, place, 0).wait_recv()
            for c in chs:
                plane_copy(group, c + q, place, 0).wait_recv()
        for i in range(1, fanout):
            other = lax.rem(place + i, fanout)
            plane_copy(group, place, other, other).wait_send()

    each(0, peers, relayed)
    each(0, peers, gathered)

    def drained(d):
        for kind in range(2):
            @pl.when(d != here)
            def _():
                for s in range(segs):
                    near_copy(kind, d, s, True).wait_send()

            @pl.when((d < here) | ((d > here) & has_head))
            def _():
                far_copy(kind, d, 0).wait_send()

    each(0, peers, drained)

    @pl.when(jnp.logical_not(top))
    def _():
        offs_copy.wait_send()


def exchange(bin_index, seg_offsets, rank_series, power_series):
    width, length = rank_series.shape
    bins = bin_index.shape[0]
    segs = seg_offsets.shape[0]
    peers = lax.axis_size("seg")
    plane = (lax.axis_size("ch"), lax.axis_size("sub"))
    fanout = plane[0] * plane[1]
    shape = (segs, 2, bins // peers, width)
    vmem = pl.BlockSpec(memory_space=pltpu.VMEM)
    smem = pl.BlockSpec(memory_space=pltpu.SMEM)
    hbm = pl.BlockSpec(memory_space=pltpu.HBM)
    dma = pltpu.SemaphoreType.DMA
    return pl.pallas_call(
        functools.partial(exchange_kernel, length, 1024, peers, plane),
        out_shape=(
            jax.ShapeDtypeStruct((fanout, peers) + shape, jnp.bfloat16),
            jax.ShapeDtypeStruct((peers,) + shape, jnp.bfloat16),
        ),
        in_specs=[vmem, smem, hbm, hbm],
        out_specs=(vmem, vmem),
        scratch_shapes=[
            pltpu.VMEM((4, length // FINE, bins), jnp.float32),
            pltpu.VMEM((2, 2 * length, bins), jnp.float32),
            pltpu.VMEM((2 * width, 2 * bins), jnp.float32),
            pltpu.VMEM((2, segs, 2, 2 * width // LANES, bins, LANES), jnp.float32),
            pltpu.SMEM((segs,), jnp.int32),
            pltpu.VMEM((2 * width, length), jnp.bfloat16),
        ]
        + [pltpu.VMEM((2, peers) + shape, jnp.bfloat16)] * 4
        + [dma((2,)), dma((2,))]
        + [dma((2, peers, segs))] * 3
        + [dma((2, peers))] * 2
        + [dma((peers, fanout))] * 2,
        compiler_params=pltpu.CompilerParams(
            vmem_limit_bytes=51 << 20, collective_id=0, has_side_effects=True
        ),
        name="exchange_spectra",
    )(bin_index[None, :], seg_offsets, rank_series, power_series)


def cross_kernel(step, rank_ref, power_ref, out_hbm, wide, stage, sem):
    gathered, depth, block, width = power_ref.shape
    per = width // LANES
    pad = wide.shape[1] // depth

    @pl.loop(0, depth)
    def _(e):
        at = pl.ds(pl.multiple_of(e * pad, 8), block)
        for l in range(per):
            lanes = slice(l * LANES, (l + 1) * LANES)
            wide[l, at, :] = rank_ref[e, :, lanes].astype(jnp.float32)
            for d in range(gathered):
                wide[per * (1 + d) + l, at, :] = power_ref[d, e, :, lanes].astype(jnp.float32)

    def copy(i):
        return pltpu.make_async_copy(stage.at[i], out_hbm.at[:, i], sem.at[i])

    def rows(first, i, t):
        return jnp.concatenate(
            [wide[first + l, pl.ds(i + t * pad, depth // 2, stride=2 * pad), :] for l in range(per)], axis=1
        )

    @pl.loop(0, block // step)
    def _(b):
        for j in range(step):
            i = b * step + j
            re, im = rows(0, i, 0), rows(0, i, 1)
            both = jnp.concatenate(
                [jnp.concatenate([re, -im], axis=1), jnp.concatenate([im, re], axis=1)], axis=0
            ).astype(jnp.bfloat16)
            for d in range(gathered):
                first = per * (1 + d)
                power = jnp.concatenate([rows(first, i, 0), rows(first, i, 1)], axis=0)
                sums = lax.dot_general(
                    both,
                    power.astype(jnp.bfloat16),
                    (((0,), (0,)), ((), ())),
                    preferred_element_type=jnp.float32,
                ).astype(stage.dtype)
                stage[i, 0, :, d * width : (d + 1) * width] = sums[:width]
                stage[i, 1, :, d * width : (d + 1) * width] = sums[width:]
            copy(i).start()

    @pl.loop(0, block)
    def _(i):
        copy(i).wait()


def cross(rank_owned, power_all):
    gathered, peers, segs, _, bins, width = power_all.shape
    depth = 2 * peers * segs
    pad = -(-bins // 8) * 8 + 8
    vmem = pl.BlockSpec(memory_space=pltpu.VMEM)
    return pl.pallas_call(
        functools.partial(cross_kernel, min(8, bins)),
        out_shape=jax.ShapeDtypeStruct((2, bins, width, gathered * width), jnp.bfloat16),
        in_specs=[vmem, vmem],
        out_specs=pl.BlockSpec(memory_space=pl.ANY),
        scratch_shapes=[
            pltpu.VMEM(((1 + gathered) * width // LANES, depth * pad, LANES), jnp.float32),
            pltpu.VMEM((bins, 2, width, gathered * width), jnp.bfloat16),
            pltpu.SemaphoreType.DMA((bins,)),
        ],
        compiler_params=pltpu.CompilerParams(vmem_limit_bytes=48 << 20),
        name="cross_spectra",
    )(rank_owned.reshape(depth, bins, width), power_all.reshape(gathered, depth, bins, width))


def body(rank_series, power_series, seg_offsets, bin_index):
    power_all, rank_owned = exchange(bin_index, seg_offsets, rank_series, power_series)
    return cross(rank_owned, power_all)


def solution(mesh):
    return jax.shard_map(
        body,
        mesh=mesh,
        in_specs=(
            P(("groups", "ch", "sub"), "seg"),
            P(("groups", "ch", "sub"), "seg"),
            P(("groups", "seg")),
            P(),
        ),
        out_specs=P(None, ("groups", "seg"), ("ch", "sub"), None),
        check_vma=False,
    )
```

```python
import functools
import math

import jax
import jax.numpy as jnp
from jax import lax
from jax.experimental import pallas as pl
from jax.experimental.pallas import tpu as pltpu
from jax.sharding import PartitionSpec as P

LANES = 128
FINE = 64
POWER, RANK = 0, 1
HEAD, OWN = 0, 1
HALVES = 2


def waves_of(freq, samples, length):
    phase = jnp.bitwise_and(freq * samples, length - 1)
    angle = 2.0 * math.pi / length * phase.astype(jnp.float32)
    return jnp.cos(angle), jnp.sin(angle)


def build_table(length, ints_ref, coarse, table):
    bins = table.shape[-1]
    pad = length // 2
    factor = (3.0 * length / 8.0) ** (-0.5)
    rows = length // FINE
    fine = lax.broadcasted_iota(jnp.int32, (FINE, bins), 0)
    steps = lax.broadcasted_iota(jnp.int32, (rows, bins), 0) * FINE
    freq = ints_ref[:, :bins]
    cb, sb = waves_of(freq, fine, length)
    cv, sv = waves_of(1, fine, length)
    cv, sv = cv * (0.5 * factor), sv * (0.5 * factor)
    coarse[0], coarse[1] = waves_of(freq, steps, length)
    coarse[2], coarse[3] = waves_of(1, steps, length)

    @pl.loop(0, rows)
    def _(a):
        ca = coarse[0, pl.ds(a, 1), :]
        sa = coarse[1, pl.ds(a, 1), :]
        cw = coarse[2, pl.ds(a, 1), :]
        sw = coarse[3, pl.ds(a, 1), :]
        window = 0.5 * factor - (cw * cv - sw * sv)
        at = pl.ds(pl.multiple_of(pad + a * FINE, FINE), FINE)
        table[0, at, :] = (ca * cb - sa * sb) * window
        table[1, at, :] = -(sa * cb + ca * sb) * window

    @pl.loop(0, pad // FINE)
    def _(a):
        for t in range(2):
            for base in (0, pad + length):
                at = pl.ds(pl.multiple_of(base + a * FINE, FINE), FINE)
                table[t, at, :] = jnp.zeros((FINE, bins), jnp.float32)


def transform(length, side, chunk, table, offset, series, acc, stage, s):
    bins = table.shape[-1]
    first = 0 if side == HEAD else length // 2
    offset = jnp.minimum(jnp.maximum(offset, length // 2), length)
    shift = (length if side == HEAD else 0) + length // 2 - offset
    acc[...] = jnp.zeros_like(acc)

    @pl.loop(0, (length - first) // chunk)
    def _(c):
        col = pl.multiple_of(first + c * chunk, chunk)
        at = pl.ds(col + shift, chunk)
        waves = jnp.concatenate(
            [table[0, at, :].astype(jnp.bfloat16), table[1, at, :].astype(jnp.bfloat16)], axis=1
        )
        acc[...] += jnp.dot(series[:, pl.ds(col, chunk)], waves, preferred_element_type=jnp.float32)

    for t in range(2):
        for l in range(acc.shape[0] // LANES):
            lanes = slice(l * LANES, (l + 1) * LANES)
            stage[side, s, t, l] = acc[lanes, t * bins : (t + 1) * bins].T


def exchange_kernel(
    length, chunk, peers, plane, ints_ref, rank_hbm, power_hbm,
    power_all, rank_owned, coarse, table, acc, stage, own_ints, head_ints, series,
    near, from_above, from_below, summed,
    load_sem, ints_sem, near_send, above_recv, below_recv, far_send, far_recv, plane_send, plane_recv,
):
    mesh_id = pl.DeviceIdType.MESH
    here = lax.axis_index("seg")
    above = lax.rem(here + 1, peers)
    below = lax.rem(here + peers - 1, peers)
    fanout = plane[0] * plane[1]
    place = lax.axis_index("ch") * plane[1] + lax.axis_index("sub")
    segs, _, block, width = summed.shape[2:]
    bins = peers * block
    half = segs // HALVES
    top = here == peers - 1
    has_head = here > 0

    loads = [
        pltpu.make_async_copy(power_hbm, series.at[pl.ds(0, width)], load_sem.at[0]),
        pltpu.make_async_copy(rank_hbm, series.at[pl.ds(width, width)], load_sem.at[1]),
        pltpu.make_async_copy(ints_ref, own_ints, load_sem.at[2]),
    ]
    for load in loads:
        load.start()

    def beside(q):
        return {"ch": q // plane[1], "sub": lax.rem(q, plane[1])}

    barrier = pltpu.get_barrier_semaphore()
    for i in range(1, peers):
        pl.semaphore_signal(
            barrier, inc=1, device_id={"seg": lax.rem(here + i, peers)}, device_id_type=mesh_id
        )
    for i in range(1, fanout):
        pl.semaphore_signal(
            barrier, inc=1, device_id=beside(lax.rem(place + i, fanout)), device_id_type=mesh_id
        )

    build_table(length, ints_ref, coarse, table)
    for load in loads:
        load.wait()
    for s in range(segs // HALVES):
        transform(length, OWN, chunk, table, own_ints[0, bins + s], series, acc, stage, s)
    pl.semaphore_wait(barrier, peers + fanout - 2)

    ints_copy = pltpu.make_async_remote_copy(
        src_ref=own_ints,
        dst_ref=head_ints,
        send_sem=ints_sem.at[0],
        recv_sem=ints_sem.at[1],
        device_id={"seg": above},
        device_id_type=mesh_id,
    )

    def near_copy(kind, owner, s, up):
        return pltpu.make_async_remote_copy(
            src_ref=near.at[kind, owner, s],
            dst_ref=(from_below if up else from_above).at[kind, owner, s],
            send_sem=near_send.at[kind, owner, s],
            recv_sem=(below_recv if up else above_recv).at[kind, owner, s],
            device_id={"seg": above if up else below},
            device_id_type=mesh_id,
        )

    def slot(kind, group):
        return power_all.at[place, group] if kind == POWER else rank_owned.at[group]

    def part(ref, h):
        return ref.at[pl.ds(h * half, half)]

    def far_copy(kind, owner, group, h):
        return pltpu.make_async_remote_copy(
            src_ref=part(summed.at[kind, owner], h),
            dst_ref=part(slot(kind, group), h),
            send_sem=far_send.at[kind, owner, h],
            recv_sem=far_recv.at[kind, group, h],
            device_id={"seg": owner},
            device_id_type=mesh_id,
        )

    def plane_copy(group, sender, target, lane):
        return pltpu.make_async_remote_copy(
            src_ref=power_all.at[sender, group],
            dst_ref=power_all.at[sender, group],
            send_sem=plane_send.at[group, lane],
            recv_sem=plane_recv.at[group, sender],
            device_id=beside(target),
            device_id_type=mesh_id,
        )

    my_ch, my_sub = lax.axis_index("ch"), lax.axis_index("sub")
    chs = [lax.rem(my_ch + i, plane[0]) * plane[1] for i in range(1, plane[0])]
    subs = [lax.rem(my_sub + i, plane[1]) for i in range(1, plane[1])]
    column = my_ch * plane[1]

    def forward(group):
        for target in [c + my_sub for c in chs] + [column + q for q in subs]:
            plane_copy(group, place, target, target).start()

    def piece(side, kind, owner, s, t):
        rows = pl.ds(pl.multiple_of(owner * block, block), block)
        per = width // LANES
        return jnp.concatenate([stage[side, s, t, kind * per + l, rows, :] for l in range(per)], axis=1)

    def send_near(side, kind, owner, s):
        for t in range(2):
            near[kind, owner, s, t] = piece(side, kind, owner, s, t).astype(near.dtype)
        near_copy(kind, owner, s, side == OWN).start()

    def total(side, kind, owner, h, late, out):
        for s in range(h * half, (h + 1) * half):
            if late is not None:
                near_copy(kind, owner, s, side == HEAD).wait_recv()
            for t in range(2):
                value = piece(side, kind, owner, s, t)
                if late is not None:
                    value = value + late[kind, owner, s, t].astype(jnp.float32)
                out[s, t] = value.astype(out.dtype)

    def own_total(kind, owner, h, out):
        @pl.when(jnp.logical_not(top))
        def _():
            total(OWN, kind, owner, h, from_above, out)

        @pl.when(top)
        def _():
            total(OWN, kind, owner, h, None, out)

    def head_total(kind, owner, h, out):
        total(HEAD, kind, owner, h, from_below, out)

    def each(low, high, step):
        lax.fori_loop(low, high, lambda d, _: step(d), None)

    def downward(high, s):
        for kind in range(2):
            each(0, high, lambda d: send_near(HEAD, kind, d, s))

    def upward(s):
        for kind in range(2):
            each(0, peers - 1 - here, lambda i: send_near(OWN, kind, peers - 1 - i, s))

    @pl.when(jnp.logical_not(top))
    def _():
        ints_copy.start()

    def total_down(kind, h, d):
        own_total(kind, d, h, summed.at[kind, d])
        far_copy(kind, d, here, h).start()

    def total_up(kind, h, i):
        d = peers - 1 - i
        head_total(kind, d, h, summed.at[kind, d])
        far_copy(kind, d, below, h).start()

    for h in range(HALVES):
        for s in range(h * half, (h + 1) * half):
            if h > 0:
                transform(length, OWN, chunk, table, own_ints[0, bins + s], series, acc, stage, s)

        @pl.when(top)
        def _():
            each(0, here - 1, functools.partial(total_down, POWER, h))

        for s in range(h * half, (h + 1) * half):
            upward(s)

    @pl.when(has_head)
    def _():
        ints_copy.wait_recv()
        for s in range(segs):
            transform(length, HEAD, chunk, table, head_ints[0, bins + s], series, acc, stage, s)
            downward(jnp.where(top, here - 1, here), s)

        @pl.when(top)
        def _():
            for kind in range(2):
                for s in range(segs):
                    send_near(HEAD, kind, here - 1, s)
            for kind in range(2):
                for h in range(HALVES):
                    total_down(kind, h, here - 1)
            for h in range(HALVES):
                each(0, here - 1, functools.partial(total_down, RANK, h))

    for kind in range(2):
        for h in range(HALVES):
            each(0, jnp.where(top, 0, here), functools.partial(total_down, kind, h))
        for h in range(HALVES):
            each(0, jnp.where(has_head, peers - 1 - here, 0), functools.partial(total_up, kind, h))

    def local(kind):
        for h in range(HALVES):
            own_total(kind, here, h, slot(kind, here))
        if kind == POWER:
            forward(here)

        @pl.when(has_head)
        def _():
            for h in range(HALVES):
                head_total(kind, here, h, slot(kind, here - 1))
            if kind == POWER:
                forward(here - 1)

    def others(step):
        each(2, here + 1, lambda i: step(here - i))

        @pl.when(jnp.logical_not(top))
        def _():
            step(peers - 1)

        each(here + 1, peers - 1, step)

    def landed(kind, group):
        for h in range(HALVES):
            far_copy(kind, here, group, h).wait_recv()

    def arrived(group):
        landed(POWER, group)
        forward(group)

    local(POWER)
    others(arrived)
    local(RANK)

    def relayed(group):
        for c in chs:
            plane_copy(group, c + my_sub, place, 0).wait_recv()
            for q in subs:
                plane_copy(group, c + my_sub, column + q, c + q).start()

    def gathered(group):
        for q in subs:
            plane_copy(group, column + q, place, 0).wait_recv()
            for c in chs:
                plane_copy(group, c + q, place, 0).wait_recv()
        for i in range(1, fanout):
            other = lax.rem(place + i, fanout)
            plane_copy(group, place, other, other).wait_send()

    each(0, peers, relayed)
    others(functools.partial(landed, RANK))
    each(0, peers, gathered)

    def drained(d):
        for kind in range(2):
            @pl.when(d != here)
            def _():
                for s in range(segs):
                    near_copy(kind, d, s, True).wait_send()

            @pl.when((d < here) | ((d > here) & has_head))
            def _():
                for h in range(HALVES):
                    far_copy(kind, d, 0, h).wait_send()

    each(0, peers, drained)

    @pl.when(jnp.logical_not(top))
    def _():
        ints_copy.wait_send()


def exchange(ints, bins, rank_series, power_series):
    width, length = rank_series.shape
    segs = ints.shape[1] - bins
    peers = lax.axis_size("seg")
    plane = (lax.axis_size("ch"), lax.axis_size("sub"))
    fanout = plane[0] * plane[1]
    shape = (segs, 2, bins // peers, width)
    vmem = pl.BlockSpec(memory_space=pltpu.VMEM)
    hbm = pl.BlockSpec(memory_space=pltpu.HBM)
    dma = pltpu.SemaphoreType.DMA
    return pl.pallas_call(
        functools.partial(exchange_kernel, length, 1024, peers, plane),
        out_shape=(
            jax.ShapeDtypeStruct((fanout, peers) + shape, jnp.bfloat16),
            jax.ShapeDtypeStruct((peers,) + shape, jnp.bfloat16),
        ),
        in_specs=[vmem, hbm, hbm],
        out_specs=(vmem, vmem),
        scratch_shapes=[
            pltpu.VMEM((4, length // FINE, bins), jnp.float32),
            pltpu.VMEM((2, 2 * length, bins), jnp.float32),
            pltpu.VMEM((2 * width, 2 * bins), jnp.float32),
            pltpu.VMEM((2, segs, 2, 2 * width // LANES, bins, LANES), jnp.float32),
            pltpu.SMEM(ints.shape, jnp.int32),
            pltpu.SMEM(ints.shape, jnp.int32),
            pltpu.VMEM((2 * width, length), jnp.bfloat16),
        ]
        + [pltpu.VMEM((2, peers) + shape, jnp.bfloat16)] * 4
        + [dma((3,)), dma((2,))]
        + [dma((2, peers, segs))] * 3
        + [dma((2, peers, HALVES))] * 2
        + [dma((peers, fanout))] * 2,
        compiler_params=pltpu.CompilerParams(
            vmem_limit_bytes=51 << 20, collective_id=0, has_side_effects=True
        ),
        name="exchange_spectra",
    )(ints, rank_series, power_series)


def cross_kernel(step, rank_ref, power_ref, out_hbm, wide, stage, sem):
    gathered, depth, block, width = power_ref.shape
    per = width // LANES
    pad = wide.shape[1] // depth

    @pl.loop(0, depth)
    def _(e):
        at = pl.ds(pl.multiple_of(e * pad, 8), block)
        for l in range(per):
            lanes = slice(l * LANES, (l + 1) * LANES)
            wide[l, at, :] = rank_ref[e, :, lanes].astype(jnp.float32)
            for d in range(gathered):
                wide[per * (1 + d) + l, at, :] = power_ref[d, e, :, lanes].astype(jnp.float32)

    def copy(i):
        return pltpu.make_async_copy(stage.at[i], out_hbm.at[:, i], sem.at[i])

    def rows(first, i, t):
        return jnp.concatenate(
            [wide[first + l, pl.ds(i + t * pad, depth // 2, stride=2 * pad), :] for l in range(per)], axis=1
        )

    @pl.loop(0, block // step)
    def _(b):
        for j in range(step):
            i = b * step + j
            re, im = rows(0, i, 0), rows(0, i, 1)
            both = jnp.concatenate(
                [jnp.concatenate([re, -im], axis=1), jnp.concatenate([im, re], axis=1)], axis=0
            ).astype(jnp.bfloat16)
            for d in range(gathered):
                first = per * (1 + d)
                power = jnp.concatenate([rows(first, i, 0), rows(first, i, 1)], axis=0)
                sums = lax.dot_general(
                    both,
                    power.astype(jnp.bfloat16),
                    (((0,), (0,)), ((), ())),
                    preferred_element_type=jnp.float32,
                ).astype(stage.dtype)
                stage[i, 0, :, d * width : (d + 1) * width] = sums[:width]
                stage[i, 1, :, d * width : (d + 1) * width] = sums[width:]
            copy(i).start()

    @pl.loop(0, block)
    def _(i):
        copy(i).wait()


def cross(rank_owned, power_all):
    gathered, peers, segs, _, bins, width = power_all.shape
    depth = 2 * peers * segs
    pad = -(-bins // 8) * 8 + 8
    vmem = pl.BlockSpec(memory_space=pltpu.VMEM)
    return pl.pallas_call(
        functools.partial(cross_kernel, min(8, bins)),
        out_shape=jax.ShapeDtypeStruct((2, bins, width, gathered * width), jnp.bfloat16),
        in_specs=[vmem, vmem],
        out_specs=pl.BlockSpec(memory_space=pl.ANY),
        scratch_shapes=[
            pltpu.VMEM(((1 + gathered) * width // LANES, depth * pad, LANES), jnp.float32),
            pltpu.VMEM((bins, 2, width, gathered * width), jnp.bfloat16),
            pltpu.SemaphoreType.DMA((bins,)),
        ],
        compiler_params=pltpu.CompilerParams(vmem_limit_bytes=48 << 20),
        name="cross_spectra",
    )(rank_owned.reshape(depth, bins, width), power_all.reshape(gathered, depth, bins, width))


def body(rank_series, power_series, seg_offsets, bin_index):
    bins = bin_index.shape[0]
    ints = jnp.concatenate([bin_index, seg_offsets])[None, :]
    power_all, rank_owned = exchange(ints, bins, rank_series, power_series)
    return cross(rank_owned, power_all)


def solution(mesh):
    return jax.shard_map(
        body,
        mesh=mesh,
        in_specs=(
            P(("groups", "ch", "sub"), "seg"),
            P(("groups", "ch", "sub"), "seg"),
            P(("groups", "seg")),
            P(),
        ),
        out_specs=P(None, ("groups", "seg"), ("ch", "sub"), None),
        check_vma=False,
    )
```

```python
import functools
import math

import jax
import jax.numpy as jnp
from jax import lax
from jax.experimental import pallas as pl
from jax.experimental.pallas import tpu as pltpu
from jax.sharding import PartitionSpec as P

LANES = 128
FINE = 64
POWER, RANK = 0, 1
HEAD, OWN = 0, 1
HALVES = 2


def waves_of(freq, samples, length):
    phase = jnp.bitwise_and(freq * samples, length - 1)
    angle = 2.0 * math.pi / length * phase.astype(jnp.float32)
    return jnp.cos(angle), jnp.sin(angle)


def start_table(length, ints_ref, coarse, fine):
    bins = fine.shape[-1]
    freq = ints_ref[:, :bins]
    within = lax.broadcasted_iota(jnp.int32, (FINE, bins), 0)
    steps = lax.broadcasted_iota(jnp.int32, (length // FINE, bins), 0) * FINE
    for k, base in enumerate((freq, 1)):
        fine[2 * k], fine[2 * k + 1] = waves_of(base, within, length)
        coarse[2 * k], coarse[2 * k + 1] = waves_of(base, steps, length)


def fill_table(length, half, coarse, fine, table):
    bins = table.shape[-1]
    pad = length // 2
    factor = (3.0 * length / 8.0) ** (-0.5)
    rows = pad // FINE
    cb, sb = fine[0], fine[1]
    cv, sv = fine[2] * (0.5 * factor), fine[3] * (0.5 * factor)

    @pl.loop(half * rows, (half + 1) * rows)
    def _(a):
        ca = coarse[0, pl.ds(a, 1), :]
        sa = coarse[1, pl.ds(a, 1), :]
        cw = coarse[2, pl.ds(a, 1), :]
        sw = coarse[3, pl.ds(a, 1), :]
        window = 0.5 * factor - (cw * cv - sw * sv)
        at = pl.ds(pl.multiple_of(pad + a * FINE, FINE), FINE)
        table[0, at, :] = (ca * cb - sa * sb) * window
        table[1, at, :] = -(sa * cb + ca * sb) * window
        at = pl.ds(pl.multiple_of(half * length + a * FINE, FINE), FINE)
        for t in range(2):
            table[t, at, :] = jnp.zeros((FINE, bins), jnp.float32)


def transform(length, side, chunk, table, offset, series, acc, stage, s):
    bins = table.shape[-1]
    first = 0 if side == HEAD else length // 2
    offset = jnp.minimum(jnp.maximum(offset, length // 2), length)
    shift = (length if side == HEAD else 0) + length // 2 - offset
    acc[...] = jnp.zeros_like(acc)

    @pl.loop(0, (length - first) // chunk)
    def _(c):
        col = pl.multiple_of(first + c * chunk, chunk)
        at = pl.ds(col + shift, chunk)
        waves = jnp.concatenate(
            [table[0, at, :].astype(jnp.bfloat16), table[1, at, :].astype(jnp.bfloat16)], axis=1
        )
        acc[...] += jnp.dot(series[:, pl.ds(col, chunk)], waves, preferred_element_type=jnp.float32)

    for t in range(2):
        for l in range(acc.shape[0] // LANES):
            lanes = slice(l * LANES, (l + 1) * LANES)
            stage[side, s, t, l] = acc[lanes, t * bins : (t + 1) * bins].T


def exchange_kernel(
    length, chunk, peers, plane, ints_ref, rank_hbm, power_hbm,
    power_all, rank_owned, coarse, fine, table, acc, stage, own_ints, head_ints, series,
    near, from_above, from_below, summed,
    load_sem, ints_sem, near_send, above_recv, below_recv, far_send, far_recv, plane_send, plane_recv,
):
    mesh_id = pl.DeviceIdType.MESH
    here = lax.axis_index("seg")
    above = lax.rem(here + 1, peers)
    below = lax.rem(here + peers - 1, peers)
    fanout = plane[0] * plane[1]
    place = lax.axis_index("ch") * plane[1] + lax.axis_index("sub")
    segs, _, block, width = summed.shape[2:]
    bins = peers * block
    half = segs // HALVES
    reach = length // 2
    top = here == peers - 1
    has_head = here > 0

    loads = [
        pltpu.make_async_copy(
            hbm.at[:, pl.ds(half * reach, reach)],
            series.at[pl.ds(kind * width, width), pl.ds(half * reach, reach)],
            load_sem.at[half, kind],
        )
        for half in (1, 0)
        for kind, hbm in enumerate((power_hbm, rank_hbm))
    ]
    loads.insert(0, pltpu.make_async_copy(ints_ref, own_ints, ints_sem.at[2]))
    for load in loads:
        load.start()

    def beside(q):
        return {"ch": q // plane[1], "sub": lax.rem(q, plane[1])}

    barrier = pltpu.get_barrier_semaphore()
    for i in range(1, peers):
        pl.semaphore_signal(
            barrier, inc=1, device_id={"seg": lax.rem(here + i, peers)}, device_id_type=mesh_id
        )
    for i in range(1, fanout):
        pl.semaphore_signal(
            barrier, inc=1, device_id=beside(lax.rem(place + i, fanout)), device_id_type=mesh_id
        )

    start_table(length, ints_ref, coarse, fine)
    fill_table(length, 0, coarse, fine, table)
    for load in loads[:3]:
        load.wait()
    for s in range(segs // HALVES):
        transform(length, OWN, chunk, table, own_ints[0, bins + s], series, acc, stage, s)
    pl.semaphore_wait(barrier, peers + fanout - 2)

    ints_copy = pltpu.make_async_remote_copy(
        src_ref=own_ints,
        dst_ref=head_ints,
        send_sem=ints_sem.at[0],
        recv_sem=ints_sem.at[1],
        device_id={"seg": above},
        device_id_type=mesh_id,
    )

    def near_copy(kind, owner, s, up):
        return pltpu.make_async_remote_copy(
            src_ref=near.at[kind, owner, s],
            dst_ref=(from_below if up else from_above).at[kind, owner, s],
            send_sem=near_send.at[kind, owner, s],
            recv_sem=(below_recv if up else above_recv).at[kind, owner, s],
            device_id={"seg": above if up else below},
            device_id_type=mesh_id,
        )

    def slot(kind, group):
        return power_all.at[place, group] if kind == POWER else rank_owned.at[group]

    def part(ref, h):
        return ref.at[pl.ds(h * half, half)]

    def far_copy(kind, owner, group, h):
        return pltpu.make_async_remote_copy(
            src_ref=part(summed.at[kind, owner], h),
            dst_ref=part(slot(kind, group), h),
            send_sem=far_send.at[kind, owner, h],
            recv_sem=far_recv.at[kind, group, h],
            device_id={"seg": owner},
            device_id_type=mesh_id,
        )

    def plane_copy(group, sender, target, lane):
        return pltpu.make_async_remote_copy(
            src_ref=power_all.at[sender, group],
            dst_ref=power_all.at[sender, group],
            send_sem=plane_send.at[group, lane],
            recv_sem=plane_recv.at[group, sender],
            device_id=beside(target),
            device_id_type=mesh_id,
        )

    my_ch, my_sub = lax.axis_index("ch"), lax.axis_index("sub")
    chs = [lax.rem(my_ch + i, plane[0]) * plane[1] for i in range(1, plane[0])]
    subs = [lax.rem(my_sub + i, plane[1]) for i in range(1, plane[1])]
    column = my_ch * plane[1]

    def forward(group):
        for target in [c + my_sub for c in chs] + [column + q for q in subs]:
            plane_copy(group, place, target, target).start()

    def piece(side, kind, owner, s, t):
        rows = pl.ds(pl.multiple_of(owner * block, block), block)
        per = width // LANES
        return jnp.concatenate([stage[side, s, t, kind * per + l, rows, :] for l in range(per)], axis=1)

    def send_near(side, kind, owner, s):
        for t in range(2):
            near[kind, owner, s, t] = piece(side, kind, owner, s, t).astype(near.dtype)
        near_copy(kind, owner, s, side == OWN).start()

    def total(side, kind, owner, h, late, out):
        for s in range(h * half, (h + 1) * half):
            if late is not None:
                near_copy(kind, owner, s, side == HEAD).wait_recv()
            for t in range(2):
                value = piece(side, kind, owner, s, t)
                if late is not None:
                    value = value + late[kind, owner, s, t].astype(jnp.float32)
                out[s, t] = value.astype(out.dtype)

    def own_total(kind, owner, h, out):
        @pl.when(jnp.logical_not(top))
        def _():
            total(OWN, kind, owner, h, from_above, out)

        @pl.when(top)
        def _():
            total(OWN, kind, owner, h, None, out)

    def head_total(kind, owner, h, out):
        total(HEAD, kind, owner, h, from_below, out)

    def each(low, high, step):
        lax.fori_loop(low, high, lambda d, _: step(d), None)

    def downward(high, kind, s):
        each(0, high, lambda d: send_near(HEAD, kind, d, s))

    def upward(s):
        for kind in range(2):
            each(0, peers - 1 - here, lambda i: send_near(OWN, kind, peers - 1 - i, s))

    @pl.when(jnp.logical_not(top))
    def _():
        ints_copy.start()

    def total_down(kind, h, d):
        own_total(kind, d, h, summed.at[kind, d])
        far_copy(kind, d, here, h).start()

    def total_up(kind, h, i):
        d = peers - 1 - i
        head_total(kind, d, h, summed.at[kind, d])
        far_copy(kind, d, below, h).start()

    for h in range(HALVES):
        for s in range(h * half, (h + 1) * half):
            if h > 0:
                transform(length, OWN, chunk, table, own_ints[0, bins + s], series, acc, stage, s)

        @pl.when(top)
        def _():
            each(0, here - 1, functools.partial(total_down, POWER, h))

        for s in range(h * half, (h + 1) * half):
            upward(s)

    @pl.when(jnp.logical_not(has_head))
    def _():
        for load in loads[3:]:
            load.wait()

    @pl.when(has_head)
    def _():
        fill_table(length, 1, coarse, fine, table)
        ints_copy.wait_recv()
        for load in loads[3:]:
            load.wait()
        for s in range(segs):
            transform(length, HEAD, chunk, table, head_ints[0, bins + s], series, acc, stage, s)
            downward(jnp.where(top, here - 1, here), POWER, s)
            downward(jnp.where(top, 0, here), RANK, s)
        for s in range(segs):
            downward(jnp.where(top, here - 1, 0), RANK, s)

        @pl.when(top)
        def _():
            for kind in range(2):
                for s in range(segs):
                    send_near(HEAD, kind, here - 1, s)
            for h in range(HALVES):
                total_down(POWER, h, here - 1)
            for h in range(HALVES):
                each(0, here - 1, functools.partial(total_down, RANK, h))
            for h in range(HALVES):
                total_down(RANK, h, here - 1)

    for kind in range(2):
        for h in range(HALVES):
            each(0, jnp.where(top, 0, here), functools.partial(total_down, kind, h))
        for h in range(HALVES):
            each(0, jnp.where(has_head, peers - 1 - here, 0), functools.partial(total_up, kind, h))

    def local(kind):
        for h in range(HALVES):
            own_total(kind, here, h, slot(kind, here))
        if kind == POWER:
            forward(here)

        @pl.when(has_head)
        def _():
            for h in range(HALVES):
                head_total(kind, here, h, slot(kind, here - 1))
            if kind == POWER:
                forward(here - 1)

    def others(step):
        each(2, here + 1, lambda i: step(here - i))

        @pl.when(jnp.logical_not(top))
        def _():
            step(peers - 1)

        each(here + 1, peers - 1, step)

    def landed(kind, group):
        for h in range(HALVES):
            far_copy(kind, here, group, h).wait_recv()

    def arrived(group):
        landed(POWER, group)
        forward(group)

    local(POWER)
    others(arrived)
    local(RANK)

    def relayed(group):
        for c in chs:
            plane_copy(group, c + my_sub, place, 0).wait_recv()
            for q in subs:
                plane_copy(group, c + my_sub, column + q, c + q).start()

    def gathered(group):
        for q in subs:
            plane_copy(group, column + q, place, 0).wait_recv()
            for c in chs:
                plane_copy(group, c + q, place, 0).wait_recv()
        for i in range(1, fanout):
            other = lax.rem(place + i, fanout)
            plane_copy(group, place, other, other).wait_send()

    each(0, peers, relayed)
    others(functools.partial(landed, RANK))
    each(0, peers, gathered)

    def drained(d):
        for kind in range(2):
            @pl.when(d != here)
            def _():
                for s in range(segs):
                    near_copy(kind, d, s, True).wait_send()

            @pl.when((d < here) | ((d > here) & has_head))
            def _():
                for h in range(HALVES):
                    far_copy(kind, d, 0, h).wait_send()

    each(0, peers, drained)

    @pl.when(jnp.logical_not(top))
    def _():
        ints_copy.wait_send()


def exchange(ints, bins, rank_series, power_series):
    width, length = rank_series.shape
    segs = ints.shape[1] - bins
    peers = lax.axis_size("seg")
    plane = (lax.axis_size("ch"), lax.axis_size("sub"))
    fanout = plane[0] * plane[1]
    shape = (segs, 2, bins // peers, width)
    vmem = pl.BlockSpec(memory_space=pltpu.VMEM)
    hbm = pl.BlockSpec(memory_space=pltpu.HBM)
    dma = pltpu.SemaphoreType.DMA
    return pl.pallas_call(
        functools.partial(exchange_kernel, length, 1024, peers, plane),
        out_shape=(
            jax.ShapeDtypeStruct((fanout, peers) + shape, jnp.bfloat16),
            jax.ShapeDtypeStruct((peers,) + shape, jnp.bfloat16),
        ),
        in_specs=[vmem, hbm, hbm],
        out_specs=(vmem, vmem),
        scratch_shapes=[
            pltpu.VMEM((4, length // FINE, bins), jnp.float32),
            pltpu.VMEM((4, FINE, bins), jnp.float32),
            pltpu.VMEM((2, 2 * length, bins), jnp.float32),
            pltpu.VMEM((2 * width, 2 * bins), jnp.float32),
            pltpu.VMEM((2, segs, 2, 2 * width // LANES, bins, LANES), jnp.float32),
            pltpu.SMEM(ints.shape, jnp.int32),
            pltpu.SMEM(ints.shape, jnp.int32),
            pltpu.VMEM((2 * width, length), jnp.bfloat16),
        ]
        + [pltpu.VMEM((2, peers) + shape, jnp.bfloat16)] * 4
        + [dma((2, 2)), dma((3,))]
        + [dma((2, peers, segs))] * 3
        + [dma((2, peers, HALVES))] * 2
        + [dma((peers, fanout))] * 2,
        compiler_params=pltpu.CompilerParams(
            vmem_limit_bytes=51 << 20, collective_id=0, has_side_effects=True
        ),
        name="exchange_spectra",
    )(ints, rank_series, power_series)


def cross_kernel(step, rank_ref, power_ref, out_hbm, wide, stage, sem):
    gathered, depth, block, width = power_ref.shape
    per = width // LANES
    pad = wide.shape[1] // depth

    @pl.loop(0, depth)
    def _(e):
        at = pl.ds(pl.multiple_of(e * pad, 8), block)
        for l in range(per):
            lanes = slice(l * LANES, (l + 1) * LANES)
            wide[l, at, :] = rank_ref[e, :, lanes].astype(jnp.float32)
            for d in range(gathered):
                wide[per * (1 + d) + l, at, :] = power_ref[d, e, :, lanes].astype(jnp.float32)

    def copy(i):
        return pltpu.make_async_copy(stage.at[i], out_hbm.at[:, i], sem.at[i])

    def rows(first, i, t):
        return jnp.concatenate(
            [wide[first + l, pl.ds(i + t * pad, depth // 2, stride=2 * pad), :] for l in range(per)], axis=1
        )

    @pl.loop(0, block // step)
    def _(b):
        for j in range(step):
            i = b * step + j
            re, im = rows(0, i, 0), rows(0, i, 1)
            both = jnp.concatenate(
                [jnp.concatenate([re, -im], axis=1), jnp.concatenate([im, re], axis=1)], axis=0
            ).astype(jnp.bfloat16)
            for d in range(gathered):
                first = per * (1 + d)
                power = jnp.concatenate([rows(first, i, 0), rows(first, i, 1)], axis=0)
                sums = lax.dot_general(
                    both,
                    power.astype(jnp.bfloat16),
                    (((0,), (0,)), ((), ())),
                    preferred_element_type=jnp.float32,
                ).astype(stage.dtype)
                stage[i, 0, :, d * width : (d + 1) * width] = sums[:width]
                stage[i, 1, :, d * width : (d + 1) * width] = sums[width:]
            copy(i).start()

    @pl.loop(0, block)
    def _(i):
        copy(i).wait()


def cross(rank_owned, power_all):
    gathered, peers, segs, _, bins, width = power_all.shape
    depth = 2 * peers * segs
    pad = -(-bins // 8) * 8 + 8
    vmem = pl.BlockSpec(memory_space=pltpu.VMEM)
    return pl.pallas_call(
        functools.partial(cross_kernel, min(8, bins)),
        out_shape=jax.ShapeDtypeStruct((2, bins, width, gathered * width), jnp.bfloat16),
        in_specs=[vmem, vmem],
        out_specs=pl.BlockSpec(memory_space=pl.ANY),
        scratch_shapes=[
            pltpu.VMEM(((1 + gathered) * width // LANES, depth * pad, LANES), jnp.float32),
            pltpu.VMEM((bins, 2, width, gathered * width), jnp.bfloat16),
            pltpu.SemaphoreType.DMA((bins,)),
        ],
        compiler_params=pltpu.CompilerParams(vmem_limit_bytes=48 << 20),
        name="cross_spectra",
    )(rank_owned.reshape(depth, bins, width), power_all.reshape(gathered, depth, bins, width))


def body(rank_series, power_series, seg_offsets, bin_index):
    bins = bin_index.shape[0]
    ints = jnp.concatenate([bin_index, seg_offsets])[None, :]
    power_all, rank_owned = exchange(ints, bins, rank_series, power_series)
    return cross(rank_owned, power_all)


def solution(mesh):
    return jax.shard_map(
        body,
        mesh=mesh,
        in_specs=(
            P(("groups", "ch", "sub"), "seg"),
            P(("groups", "ch", "sub"), "seg"),
            P(("groups", "seg")),
            P(),
        ),
        out_specs=P(None, ("groups", "seg"), ("ch", "sub"), None),
        check_vma=False,
    )
```

```python
import functools
import math

import jax
import jax.numpy as jnp
from jax import lax
from jax.experimental import pallas as pl
from jax.experimental.pallas import tpu as pltpu
from jax.sharding import PartitionSpec as P

LANES = 128
FINE = 64
POWER, RANK = 0, 1
HEAD, OWN = 0, 1
HALVES = 2


def waves_of(freq, samples, length):
    phase = jnp.bitwise_and(freq * samples, length - 1)
    angle = 2.0 * math.pi / length * phase.astype(jnp.float32)
    return jnp.cos(angle), jnp.sin(angle)


def start_table(length, ints_ref, coarse, fine):
    bins = fine.shape[-1]
    freq = ints_ref[:, :bins]
    within = lax.broadcasted_iota(jnp.int32, (FINE, bins), 0)
    steps = lax.broadcasted_iota(jnp.int32, (length // FINE, bins), 0) * FINE
    for k, base in enumerate((freq, 1)):
        fine[2 * k], fine[2 * k + 1] = waves_of(base, within, length)
        coarse[2 * k], coarse[2 * k + 1] = waves_of(base, steps, length)


def fill_table(length, half, coarse, fine, table):
    bins = table.shape[-1]
    pad = length // 2
    factor = (3.0 * length / 8.0) ** (-0.5)
    rows = pad // FINE
    cb, sb = fine[0], fine[1]
    cv, sv = fine[2] * (0.5 * factor), fine[3] * (0.5 * factor)

    @pl.loop(half * rows, (half + 1) * rows)
    def _(a):
        ca = coarse[0, pl.ds(a, 1), :]
        sa = coarse[1, pl.ds(a, 1), :]
        cw = coarse[2, pl.ds(a, 1), :]
        sw = coarse[3, pl.ds(a, 1), :]
        window = 0.5 * factor - (cw * cv - sw * sv)
        at = pl.ds(pl.multiple_of(pad + a * FINE, FINE), FINE)
        table[0, at, :] = (ca * cb - sa * sb) * window
        table[1, at, :] = -(sa * cb + ca * sb) * window
        at = pl.ds(pl.multiple_of(half * length + a * FINE, FINE), FINE)
        for t in range(2):
            table[t, at, :] = jnp.zeros((FINE, bins), jnp.float32)


def transform(length, side, chunk, table, offset, series, acc, stage, s):
    bins = table.shape[-1]
    first = 0 if side == HEAD else length // 2
    offset = jnp.minimum(jnp.maximum(offset, length // 2), length)
    shift = (length if side == HEAD else 0) + length // 2 - offset
    acc[...] = jnp.zeros_like(acc)

    @pl.loop(0, (length - first) // chunk)
    def _(c):
        col = pl.multiple_of(first + c * chunk, chunk)
        at = pl.ds(col + shift, chunk)
        waves = jnp.concatenate(
            [table[0, at, :].astype(jnp.bfloat16), table[1, at, :].astype(jnp.bfloat16)], axis=1
        )
        acc[...] += jnp.dot(series[:, pl.ds(col, chunk)], waves, preferred_element_type=jnp.float32)

    for t in range(2):
        for l in range(acc.shape[0] // LANES):
            lanes = slice(l * LANES, (l + 1) * LANES)
            stage[side, s, t, l] = acc[lanes, t * bins : (t + 1) * bins].T


def row_pitch(block):
    return -(-block // 8) * 8 + 8


def spread(power_all, power_rows):
    senders, peers, segs, _, block, width = power_all.shape
    per = width // LANES

    @pl.loop(0, peers)
    def _(group):
        for s in range(segs):
            for t in range(2):
                start = ((group * segs + s) * 2 + t) * row_pitch(block)
                at = pl.ds(pl.multiple_of(start, 8), block)
                for d in range(senders):
                    for l in range(per):
                        piece = power_all[d, group, s, t, :, l * LANES : (l + 1) * LANES]
                        power_rows[d][l, at, :] = piece.astype(jnp.float32)


def exchange_kernel(
    length, chunk, peers, plane, ints_ref, rank_hbm, power_hbm, *refs,
):
    fanout = plane[0] * plane[1]
    power_rows = refs[:fanout]
    (
        rank_owned, power_all, coarse, fine, table, acc, stage, own_ints, head_ints, series,
    near, from_above, from_below, summed,
    load_sem, ints_sem, near_send, above_recv, below_recv, far_send, far_recv, plane_send, plane_recv,
    ) = refs[fanout:]
    mesh_id = pl.DeviceIdType.MESH
    here = lax.axis_index("seg")
    above = lax.rem(here + 1, peers)
    below = lax.rem(here + peers - 1, peers)
    fanout = plane[0] * plane[1]
    place = lax.axis_index("ch") * plane[1] + lax.axis_index("sub")
    segs, _, block, width = summed.shape[2:]
    bins = peers * block
    half = segs // HALVES
    reach = length // 2
    top = here == peers - 1
    has_head = here > 0

    loads = [
        pltpu.make_async_copy(
            hbm.at[:, pl.ds(half * reach, reach)],
            series.at[pl.ds(kind * width, width), pl.ds(half * reach, reach)],
            load_sem.at[half, kind],
        )
        for half in (1, 0)
        for kind, hbm in enumerate((power_hbm, rank_hbm))
    ]
    loads.insert(0, pltpu.make_async_copy(ints_ref, own_ints, ints_sem.at[2]))
    for load in loads:
        load.start()

    def beside(q):
        return {"ch": q // plane[1], "sub": lax.rem(q, plane[1])}

    barrier = pltpu.get_barrier_semaphore()
    for i in range(1, peers):
        pl.semaphore_signal(
            barrier, inc=1, device_id={"seg": lax.rem(here + i, peers)}, device_id_type=mesh_id
        )
    for i in range(1, fanout):
        pl.semaphore_signal(
            barrier, inc=1, device_id=beside(lax.rem(place + i, fanout)), device_id_type=mesh_id
        )

    start_table(length, ints_ref, coarse, fine)
    fill_table(length, 0, coarse, fine, table)
    for load in loads[:3]:
        load.wait()
    for s in range(segs // HALVES):
        transform(length, OWN, chunk, table, own_ints[0, bins + s], series, acc, stage, s)
    pl.semaphore_wait(barrier, peers + fanout - 2)

    ints_copy = pltpu.make_async_remote_copy(
        src_ref=own_ints,
        dst_ref=head_ints,
        send_sem=ints_sem.at[0],
        recv_sem=ints_sem.at[1],
        device_id={"seg": above},
        device_id_type=mesh_id,
    )

    def near_copy(kind, owner, s, up):
        return pltpu.make_async_remote_copy(
            src_ref=near.at[kind, owner, s],
            dst_ref=(from_below if up else from_above).at[kind, owner, s],
            send_sem=near_send.at[kind, owner, s],
            recv_sem=(below_recv if up else above_recv).at[kind, owner, s],
            device_id={"seg": above if up else below},
            device_id_type=mesh_id,
        )

    def slot(kind, group):
        return power_all.at[place, group] if kind == POWER else rank_owned.at[group]

    def part(ref, h):
        return ref.at[pl.ds(h * half, half)]

    def far_copy(kind, owner, group, h):
        return pltpu.make_async_remote_copy(
            src_ref=part(summed.at[kind, owner], h),
            dst_ref=part(slot(kind, group), h),
            send_sem=far_send.at[kind, owner, h],
            recv_sem=far_recv.at[kind, group, h],
            device_id={"seg": owner},
            device_id_type=mesh_id,
        )

    def plane_copy(group, sender, target, lane):
        return pltpu.make_async_remote_copy(
            src_ref=power_all.at[sender, group],
            dst_ref=power_all.at[sender, group],
            send_sem=plane_send.at[group, lane],
            recv_sem=plane_recv.at[group, sender],
            device_id=beside(target),
            device_id_type=mesh_id,
        )

    my_ch, my_sub = lax.axis_index("ch"), lax.axis_index("sub")
    chs = [lax.rem(my_ch + i, plane[0]) * plane[1] for i in range(1, plane[0])]
    subs = [lax.rem(my_sub + i, plane[1]) for i in range(1, plane[1])]
    column = my_ch * plane[1]

    def forward(group):
        for target in [c + my_sub for c in chs] + [column + q for q in subs]:
            plane_copy(group, place, target, target).start()

    def piece(side, kind, owner, s, t):
        rows = pl.ds(pl.multiple_of(owner * block, block), block)
        per = width // LANES
        return jnp.concatenate([stage[side, s, t, kind * per + l, rows, :] for l in range(per)], axis=1)

    def send_near(side, kind, owner, s):
        for t in range(2):
            near[kind, owner, s, t] = piece(side, kind, owner, s, t).astype(near.dtype)
        near_copy(kind, owner, s, side == OWN).start()

    def total(side, kind, owner, h, late, out):
        for s in range(h * half, (h + 1) * half):
            if late is not None:
                near_copy(kind, owner, s, side == HEAD).wait_recv()
            for t in range(2):
                value = piece(side, kind, owner, s, t)
                if late is not None:
                    value = value + late[kind, owner, s, t].astype(jnp.float32)
                out[s, t] = value.astype(out.dtype)

    def own_total(kind, owner, h, out):
        @pl.when(jnp.logical_not(top))
        def _():
            total(OWN, kind, owner, h, from_above, out)

        @pl.when(top)
        def _():
            total(OWN, kind, owner, h, None, out)

    def head_total(kind, owner, h, out):
        total(HEAD, kind, owner, h, from_below, out)

    def each(low, high, step):
        lax.fori_loop(low, high, lambda d, _: step(d), None)

    def downward(high, kind, s):
        each(0, high, lambda d: send_near(HEAD, kind, d, s))

    def upward(s):
        for kind in range(2):
            each(0, peers - 1 - here, lambda i: send_near(OWN, kind, peers - 1 - i, s))

    @pl.when(jnp.logical_not(top))
    def _():
        ints_copy.start()

    def total_down(kind, h, d):
        own_total(kind, d, h, summed.at[kind, d])
        far_copy(kind, d, here, h).start()

    def total_up(kind, h, i):
        d = peers - 1 - i
        head_total(kind, d, h, summed.at[kind, d])
        far_copy(kind, d, below, h).start()

    for h in range(HALVES):
        for s in range(h * half, (h + 1) * half):
            if h > 0:
                transform(length, OWN, chunk, table, own_ints[0, bins + s], series, acc, stage, s)

        @pl.when(top)
        def _():
            each(0, here - 1, functools.partial(total_down, POWER, h))

        for s in range(h * half, (h + 1) * half):
            upward(s)

    @pl.when(jnp.logical_not(has_head))
    def _():
        for load in loads[3:]:
            load.wait()

    @pl.when(has_head)
    def _():
        fill_table(length, 1, coarse, fine, table)
        ints_copy.wait_recv()
        for load in loads[3:]:
            load.wait()
        for s in range(segs):
            transform(length, HEAD, chunk, table, head_ints[0, bins + s], series, acc, stage, s)
            downward(jnp.where(top, here - 1, here), POWER, s)
            downward(jnp.where(top, 0, here), RANK, s)
        for s in range(segs):
            downward(jnp.where(top, here - 1, 0), RANK, s)

        @pl.when(top)
        def _():
            for kind in range(2):
                for s in range(segs):
                    send_near(HEAD, kind, here - 1, s)
            for h in range(HALVES):
                total_down(POWER, h, here - 1)
            for h in range(HALVES):
                each(0, here - 1, functools.partial(total_down, RANK, h))
            for h in range(HALVES):
                total_down(RANK, h, here - 1)

    for kind in range(2):
        for h in range(HALVES):
            each(0, jnp.where(top, 0, here), functools.partial(total_down, kind, h))
        for h in range(HALVES):
            each(0, jnp.where(has_head, peers - 1 - here, 0), functools.partial(total_up, kind, h))

    def local(kind):
        for h in range(HALVES):
            own_total(kind, here, h, slot(kind, here))
        if kind == POWER:
            forward(here)

        @pl.when(has_head)
        def _():
            for h in range(HALVES):
                head_total(kind, here, h, slot(kind, here - 1))
            if kind == POWER:
                forward(here - 1)

    def others(step):
        each(2, here + 1, lambda i: step(here - i))

        @pl.when(jnp.logical_not(top))
        def _():
            step(peers - 1)

        each(here + 1, peers - 1, step)

    def landed(kind, group):
        for h in range(HALVES):
            far_copy(kind, here, group, h).wait_recv()

    def arrived(group):
        landed(POWER, group)
        forward(group)

    local(POWER)
    others(arrived)
    local(RANK)

    def relayed(group):
        for c in chs:
            plane_copy(group, c + my_sub, place, 0).wait_recv()
            for q in subs:
                plane_copy(group, c + my_sub, column + q, c + q).start()

    def gathered(group):
        for q in subs:
            plane_copy(group, column + q, place, 0).wait_recv()
            for c in chs:
                plane_copy(group, c + q, place, 0).wait_recv()
        for i in range(1, fanout):
            other = lax.rem(place + i, fanout)
            plane_copy(group, place, other, other).wait_send()

    each(0, peers, relayed)
    each(0, peers, gathered)
    spread(power_all, power_rows)
    others(functools.partial(landed, RANK))

    def drained(d):
        for kind in range(2):
            @pl.when(d != here)
            def _():
                for s in range(segs):
                    near_copy(kind, d, s, True).wait_send()

            @pl.when((d < here) | ((d > here) & has_head))
            def _():
                for h in range(HALVES):
                    far_copy(kind, d, 0, h).wait_send()

    each(0, peers, drained)

    @pl.when(jnp.logical_not(top))
    def _():
        ints_copy.wait_send()


def exchange(ints, bins, rank_series, power_series):
    width, length = rank_series.shape
    segs = ints.shape[1] - bins
    peers = lax.axis_size("seg")
    plane = (lax.axis_size("ch"), lax.axis_size("sub"))
    fanout = plane[0] * plane[1]
    shape = (segs, 2, bins // peers, width)
    pitched = peers * segs * 2 * row_pitch(bins // peers)
    vmem = pl.BlockSpec(memory_space=pltpu.VMEM)
    hbm = pl.BlockSpec(memory_space=pltpu.HBM)
    dma = pltpu.SemaphoreType.DMA
    return pl.pallas_call(
        functools.partial(exchange_kernel, length, 2048, peers, plane),
        out_shape=(
            *[jax.ShapeDtypeStruct((width // LANES, pitched, LANES), jnp.float32)] * fanout,
            jax.ShapeDtypeStruct((peers,) + shape, jnp.bfloat16),
        ),
        in_specs=[vmem, hbm, hbm],
        out_specs=(vmem,) * (fanout + 1),
        scratch_shapes=[
            pltpu.VMEM((fanout, peers) + shape, jnp.bfloat16),
            pltpu.VMEM((4, length // FINE, bins), jnp.float32),
            pltpu.VMEM((4, FINE, bins), jnp.float32),
            pltpu.VMEM((2, 2 * length, bins), jnp.float32),
            pltpu.VMEM((2 * width, 2 * bins), jnp.float32),
            pltpu.VMEM((2, segs, 2, 2 * width // LANES, bins, LANES), jnp.float32),
            pltpu.SMEM(ints.shape, jnp.int32),
            pltpu.SMEM(ints.shape, jnp.int32),
            pltpu.VMEM((2 * width, length), jnp.bfloat16),
        ]
        + [pltpu.VMEM((2, peers) + shape, jnp.bfloat16)] * 4
        + [dma((2, 2)), dma((3,))]
        + [dma((2, peers, segs))] * 3
        + [dma((2, peers, HALVES))] * 2
        + [dma((peers, fanout))] * 2,
        compiler_params=pltpu.CompilerParams(
            vmem_limit_bytes=48 << 20, collective_id=0, has_side_effects=True
        ),
        name="exchange_spectra",
    )(ints, rank_series, power_series)


def cross_kernel(step, rank_ref, *refs):
    *power_rows, out_hbm, rank_rows, stage, sem = refs
    depth, block, width = rank_ref.shape
    per = width // LANES
    pad = row_pitch(block)

    @pl.loop(0, depth)
    def _(e):
        at = pl.ds(pl.multiple_of(e * pad, 8), block)
        for l in range(per):
            rank_rows[l, at, :] = rank_ref[e, :, l * LANES : (l + 1) * LANES].astype(jnp.float32)

    def copy(i):
        return pltpu.make_async_copy(stage.at[i], out_hbm.at[:, i], sem.at[i])

    def rows(ref, i, t):
        at = pl.ds(i + t * pad, depth // 2, stride=2 * pad)
        return jnp.concatenate([ref[l, at, :] for l in range(per)], axis=1)

    @pl.loop(0, block // step)
    def _(b):
        for j in range(step):
            i = b * step + j
            re, im = rows(rank_rows, i, 0), rows(rank_rows, i, 1)
            both = jnp.concatenate(
                [jnp.concatenate([re, -im], axis=1), jnp.concatenate([im, re], axis=1)], axis=0
            ).astype(jnp.bfloat16)
            for d in range(len(power_rows)):
                power = jnp.concatenate([rows(power_rows[d], i, t) for t in range(2)], axis=0)
                sums = lax.dot_general(
                    both,
                    power.astype(jnp.bfloat16),
                    (((0,), (0,)), ((), ())),
                    preferred_element_type=jnp.float32,
                ).astype(stage.dtype)
                stage[i, 0, :, d * width : (d + 1) * width] = sums[:width]
                stage[i, 1, :, d * width : (d + 1) * width] = sums[width:]
            copy(i).start()

    @pl.loop(0, block)
    def _(i):
        copy(i).wait()


def cross(rank_owned, power_rows):
    peers, segs, _, bins, width = rank_owned.shape
    depth = 2 * peers * segs
    powers = len(power_rows) * width
    vmem = pl.BlockSpec(memory_space=pltpu.VMEM)
    return pl.pallas_call(
        functools.partial(cross_kernel, min(8, bins)),
        out_shape=jax.ShapeDtypeStruct((2, bins, width, powers), jnp.bfloat16),
        in_specs=[vmem] * (1 + len(power_rows)),
        out_specs=pl.BlockSpec(memory_space=pl.ANY),
        scratch_shapes=[
            pltpu.VMEM((width // LANES, power_rows[0].shape[1], LANES), jnp.float32),
            pltpu.VMEM((bins, 2, width, powers), jnp.bfloat16),
            pltpu.SemaphoreType.DMA((bins,)),
        ],
        compiler_params=pltpu.CompilerParams(vmem_limit_bytes=44 << 20),
        name="cross_spectra",
    )(rank_owned.reshape(depth, bins, width), *power_rows)


def body(rank_series, power_series, seg_offsets, bin_index):
    bins = bin_index.shape[0]
    ints = jnp.concatenate([bin_index, seg_offsets])[None, :]
    *power_rows, rank_owned = exchange(ints, bins, rank_series, power_series)
    return cross(rank_owned, power_rows)


def solution(mesh):
    return jax.shard_map(
        body,
        mesh=mesh,
        in_specs=(
            P(("groups", "ch", "sub"), "seg"),
            P(("groups", "ch", "sub"), "seg"),
            P(("groups", "seg")),
            P(),
        ),
        out_specs=P(None, ("groups", "seg"), ("ch", "sub"), None),
        check_vma=False,
    )
```
